32 devices in a mesh: gx: 4 (over y, x), gy: 8 (over z, core).
Axes of the slice: x: 2, y: 2, z: 4, core: 2. Of those that a mesh axis runs over, the one named last changes fastest.
Arguments:
- frames: bfloat16 [32, 1024, 512], P(None, ('gx', 'gy')), may hold values from -6 to 6
- skip_frames: bfloat16 [32, 1024, 512], P(None, ('gx', 'gy')), may hold values from -6 to 6
- output_grad: bfloat16 [32, 1024, 512], P(None, ('gx', 'gy')), may hold values from -6 to 6
- lengths: int32 [192], replicated, may hold values from 0 to 768, as said below
- assignment: int32 [192], replicated, may hold values from 0 to 31, as said below
- infill: int32 [32, 1024], P(('gx', 'gy')), may hold values from 0 to 1
- skip_weight: bfloat16 [1024, 512], replicated, may hold values from -0.1875 to 0.1875
- skip_bias: float32 [512], replicated, may hold values from -1.5 to 1.5
- attn_gain: float32 [512], replicated, may hold values from 0.25 to 1.75
- attn_shift: float32 [512], replicated, may hold values from -1.5 to 1.5
- qkv_weight: bfloat16 [512, 1536], replicated, may hold values from -0.25 to 0.25
- proj_weight: bfloat16 [512, 512], replicated, may hold values from -0.75 to 0.75
- proj_bias: float32 [512], replicated, may hold values from -1.5 to 1.5
- ffn_gain: float32 [512], replicated, may hold values from 0.25 to 1.75
- ffn_shift: float32 [512], replicated, may hold values from -1.5 to 1.5
- up_weight: bfloat16 [512, 2048], replicated, may hold values from -0.25 to 0.25
- up_bias: float32 [2048], replicated, may hold values from -2.5 to 2.5
- down_weight: bfloat16 [2048, 512], replicated, may hold values from -0.125 to 0.125
- down_bias: float32 [512], replicated, may hold values from -1.5 to 1.5
Outputs:
- result_frames: bfloat16 [32, 1024, 512], P(None, ('gx', 'gy'))
- frames_grad: bfloat16 [32, 1024, 512], P(None, ('gx', 'gy'))
- skip_grad: bfloat16 [32, 1024, 512], P(None, ('gx', 'gy'))
- skip_weight_grad: float32 [1024, 512], replicated
- skip_bias_grad: float32 [512], replicated
- attn_gain_grad: float32 [512], replicated
- attn_shift_grad: float32 [512], replicated
- qkv_weight_grad: float32 [512, 1536], replicated
- proj_weight_grad: float32 [512, 512], replicated
- proj_bias_grad: float32 [512], replicated
- ffn_gain_grad: float32 [512], replicated
- ffn_shift_grad: float32 [512], replicated
- up_weight_grad: float32 [512, 2048], replicated
- up_bias_grad: float32 [2048], replicated
- down_weight_grad: float32 [2048, 512], replicated
- down_bias_grad: float32 [512], replicated
The draws below stay inside these ranges and needn't reach their ends.
Inputs may be any that keep to these rules, and one draw needn't show every extreme that they name: `lengths`: A 0 marks an unused entry. The utterances of one pack have at most 1024 frames together; in every draw at least one utterance has exactly 768 frames, and every used entry of another length has 64 to 256 frames. `assignment`: each pack is named by exactly 6 entries.
All inputs are finite; a program needn't handle non-finite values.
Results may differ from the reference program's by a relative error of at most 0.014.
Values may be sent and summed in bfloat16 or wider, within the bound.
A program may use at most 256 MiB of HBM per device.

```python
from functools import partial
import jax
import jax.numpy as jnp
from jax import lax

D = 512
HEADS = 8
HEAD_DIM = 64
FF = 2048
PACK = 1024
UPP = 6
PACKS = 32
LMAX = 768
LSHORT = 256
LMIN = 64


def utterance_plan(key):
    base = jax.random.fold_in(key, 7)
    draw_common, draw_long, draw_forced, draw_shuffle = jax.random.split(base, 4)
    common_sizes = jax.random.randint(draw_common, (PACKS, UPP), LMIN, LSHORT + 1)
    picked = jax.random.randint(draw_long, (PACKS,), 0, 8) == 0
    forced = jax.random.randint(draw_forced, (), 0, PACKS)
    longer = picked | (jnp.arange(PACKS) == forced)
    leading = jnp.where(longer, LMAX, common_sizes[:, 0])
    lengths_table = jnp.concatenate([leading[:, None], common_sizes[:, 1:]], axis=1)
    running = jnp.cumsum(lengths_table, axis=1)
    retained = jnp.where(running <= PACK, lengths_table, 0)
    owners = jnp.broadcast_to(jnp.arange(PACKS)[:, None], (PACKS, UPP))
    shuffle = jax.random.permutation(draw_shuffle, PACKS * UPP)
    return (retained.reshape(-1)[shuffle].astype(jnp.int32), owners.reshape(-1)[shuffle].astype(jnp.int32))


def draw_lengths(key, part):
    return utterance_plan(key)[0]


def draw_assignment(key, part):
    return utterance_plan(key)[1]


def draw_infill(key, part):
    chance = 250 + 700 * jnp.arange(PACKS) // max(PACKS - 1, 1)
    rolls = jax.random.randint(jax.random.fold_in(key, 3), (PACKS, PACK), 0, 1000)
    return (rolls < chance[:, None]).astype(jnp.int32)


def shard_levels(rng, shape, cuts, least, high):
    gain, own = 1.0, jax.random.fold_in(rng, 6)
    for axis_at, parts in cuts:
        steps = jnp.exp(jax.random.uniform(jax.random.fold_in(own, axis_at), (parts,), jnp.float32, least / len(cuts), high / len(cuts)))
        gain = gain * jnp.repeat(steps, shape[axis_at] // parts).reshape([-1 if axis == axis_at else 1 for axis in range(len(shape))])
    return gain


def normal_values(key, extent, scale, reach, cuts=(), kind=jnp.bfloat16):
    level = shard_levels(key, extent, cuts, -0.22, 0.18) if cuts else 1.0
    values = jax.random.normal(key, extent, jnp.float32) * scale * level
    return jnp.minimum(jnp.maximum(values, -reach), reach).astype(kind)


def setup_inputs(seed: int = 0) -> dict:
    streams_of = jax.random.split(jax.random.key(seed), 20)
    frames = normal_values(streams_of[0], (PACKS, PACK, D), 1.0, 6.0, ((1, 32),))
    skip_frames = normal_values(streams_of[1], (PACKS, PACK, D), 1.0, 6.0, ((1, 32),))
    output_grad = normal_values(streams_of[2], (PACKS, PACK, D), 1.0, 6.0, ((1, 32),))
    lengths = draw_lengths(jax.random.fold_in(streams_of[19], 71), 0)
    assignment = draw_assignment(jax.random.fold_in(streams_of[19], 71), 0)
    infill = draw_infill(jax.random.fold_in(streams_of[19], 71), 0)
    skip_weight = normal_values(streams_of[6], (2 * D, D), (2 * D) ** -0.5, 0.1875)
    skip_bias = normal_values(streams_of[7], (D,), 0.3, 1.5, (), jnp.float32)
    attn_gain = jnp.clip(1.0 + 0.15 * jax.random.normal(streams_of[8], (D,), jnp.float32), 0.25, 1.75)
    attn_shift = normal_values(streams_of[9], (D,), 0.3, 1.5, (), jnp.float32)
    qkv_weight = normal_values(streams_of[10], (D, 3 * D), D ** -0.5, 0.25)
    proj_weight = normal_values(streams_of[11], (D, D), (D // 8) ** -0.5, 0.75)
    proj_bias = normal_values(streams_of[12], (D,), 0.3, 1.5, (), jnp.float32)
    ffn_gain = jnp.clip(1.0 + 0.15 * jax.random.normal(streams_of[13], (D,), jnp.float32), 0.25, 1.75)
    ffn_shift = normal_values(streams_of[14], (D,), 0.3, 1.5, (), jnp.float32)
    up_weight = normal_values(streams_of[15], (D, FF), D ** -0.5, 0.25)
    up_bias = normal_values(streams_of[16], (FF,), 0.5, 2.5, (), jnp.float32)
    down_weight = normal_values(streams_of[17], (FF, D), FF ** -0.5, 0.125)
    down_bias = normal_values(streams_of[18], (D,), 0.3, 1.5, (), jnp.float32)
    return dict(frames=frames, skip_frames=skip_frames, output_grad=output_grad, lengths=lengths, assignment=assignment, infill=infill, skip_weight=skip_weight, skip_bias=skip_bias, attn_gain=attn_gain, attn_shift=attn_shift, qkv_weight=qkv_weight, proj_weight=proj_weight, proj_bias=proj_bias, ffn_gain=ffn_gain, ffn_shift=ffn_shift, up_weight=up_weight, up_bias=up_bias, down_weight=down_weight, down_bias=down_bias)


@jax.custom_vjp
def low(v):
    return lax.optimization_barrier(v.astype(jnp.bfloat16)).astype(jnp.float32)

@jax.custom_vjp
def low_back(v):
    return v

def low_keep(v):
    return (low(v), None)

def low_pass(kept, grad):
    return (grad,)

def back_keep(v):
    return (v, None)

def back_low(kept, grad):
    return (low(grad),)
low.defvjp(low_keep, low_pass)
low_back.defvjp(back_keep, back_low)
EPSILON = 1e-05
HIGHEST = lax.Precision.HIGHEST

def layer_norm(rows_in, gain_vec, shift_vec):
    center = lax.optimization_barrier(jnp.mean(rows_in, axis=-1, keepdims=True))
    offset = rows_in - center
    spread = lax.optimization_barrier(jnp.mean(offset * offset, axis=-1, keepdims=True))
    return offset * lax.rsqrt(spread + EPSILON) * gain_vec + shift_vec

def pack_labels(lengths, assignment, frames_count, pack_id):
    member = (assignment == pack_id).astype(jnp.int32)
    in_pack = lengths * member
    starts = jnp.cumsum(in_pack, dtype=jnp.int32) - in_pack
    places = jnp.arange(frames_count, dtype=jnp.int32)
    inside = (places[None, :] >= starts[:, None]) & (places[None, :] < (starts + in_pack)[:, None])
    numbers = jnp.arange(1, in_pack.shape[0] + 1, dtype=jnp.int32)
    return lax.optimization_barrier(jnp.sum(jnp.where(inside, numbers[:, None], 0), axis=0)).astype(jnp.int32)

def block_scores(products, labels, row_start, score_scale):
    head_count = products.shape[0]
    block_rows = products.shape[1]
    key_count = products.shape[2]
    query_places = row_start + jnp.arange(block_rows, dtype=jnp.int32)
    key_places = jnp.arange(key_count, dtype=jnp.int32)
    distance = jnp.abs(query_places[:, None] - key_places[None, :]).astype(jnp.float32)
    slopes = 2.0 ** (-8.0 * jnp.arange(1, head_count + 1, dtype=jnp.float32) / head_count)
    scores = products * score_scale - slopes[:, None, None] * distance[None]
    query_labels = lax.dynamic_slice_in_dim(labels, row_start, block_rows)
    same_utt = query_labels[:, None] == labels[None, :]
    return jnp.where(same_utt[None], scores, -jnp.inf)

def attend_block(qkv_all, labels, row_start):
    model_width = qkv_all.shape[1] // 3
    frame_total = qkv_all.shape[0]
    block_rows = min(512, frame_total)
    queries = lax.dynamic_slice_in_dim(qkv_all, row_start, block_rows, 0)[:, :model_width].reshape(block_rows, HEADS, HEAD_DIM)
    key_rows = qkv_all[:, model_width:2 * model_width].reshape(frame_total, HEADS, HEAD_DIM)
    values = qkv_all[:, 2 * model_width:].reshape(frame_total, HEADS, HEAD_DIM)
    products = low_back(jnp.einsum('qhd,khd->hqk', queries, key_rows, precision=HIGHEST))
    scores = block_scores(products, labels, row_start, HEAD_DIM ** (-0.5))
    soft_low = low(jax.nn.softmax(scores, axis=-1))
    blended = jnp.einsum('hqk,khd->qhd', soft_low, values, precision=HIGHEST)
    return blended.reshape(block_rows, model_width)

def layer_forward(params, inputs, skip_in, labels, valid_rows):
    skip_weight, skip_bias, attn_gain, attn_shift, qkv_weight, proj_weight, proj_bias, ffn_gain, ffn_shift, up_weight, up_bias, down_weight, down_bias = params
    frame_total = inputs.shape[0]
    block_rows = min(512, frame_total)
    joined = jnp.concatenate([inputs, skip_in], axis=1)
    stream = low_back(jnp.dot(joined, skip_weight, precision=HIGHEST) + skip_bias)
    normed_one = low(layer_norm(stream, attn_gain, attn_shift))
    qkv_all = low(low_back(jnp.dot(normed_one, qkv_weight, precision=HIGHEST)))
    block_starts = jnp.arange(frame_total // block_rows, dtype=jnp.int32) * block_rows
    pieces = lax.map(jax.checkpoint(partial(attend_block, qkv_all, labels)), block_starts)
    blended = low(low_back(pieces.reshape(frame_total, -1)))
    projected = low_back(jnp.dot(blended, proj_weight, precision=HIGHEST) + proj_bias)
    after_attn = stream + projected
    normed_two = low(layer_norm(after_attn, ffn_gain, ffn_shift))
    pre_act = low_back(jnp.dot(normed_two, up_weight, precision=HIGHEST) + up_bias)
    hidden = low(jax.nn.gelu(pre_act, approximate=False))
    branch = low_back(jnp.dot(hidden, down_weight, precision=HIGHEST) + down_bias)
    return (after_attn + branch) * valid_rows[:, None]

def reference(frames, skip_frames, output_grad, lengths, assignment, infill, skip_weight, skip_bias, attn_gain, attn_shift, qkv_weight, proj_weight, proj_bias, ffn_gain, ffn_shift, up_weight, up_bias, down_weight, down_bias):
    labels_all = lax.map(partial(pack_labels, lengths, assignment, PACK), jnp.arange(PACKS, dtype=jnp.int32))
    valid_all = (labels_all > 0).astype(jnp.float32)
    weighting_all = infill.astype(jnp.float32) * valid_all
    factor = PACKS * PACK / jnp.sum(weighting_all)
    params = tuple((member.astype(jnp.float32) for member in (skip_weight, skip_bias, attn_gain, attn_shift, qkv_weight, proj_weight, proj_bias, ffn_gain, ffn_shift, up_weight, up_bias, down_weight, down_bias)))

    def one_pack(totals, pack_items):
        pack_frames, pack_skip, pack_grad, labels, weighting = pack_items
        valid_rows = (labels > 0).astype(jnp.float32)
        result, pull_back = jax.vjp(partial(layer_forward, labels=labels, valid_rows=valid_rows), params, pack_frames.astype(jnp.float32), pack_skip.astype(jnp.float32))
        seed_grad = pack_grad.astype(jnp.float32) * weighting[:, None] * factor
        grad_params, grad_inputs, grad_skip = pull_back(seed_grad)
        totals = jax.tree.map(jnp.add, totals, grad_params)
        return (totals, (result.astype(jnp.bfloat16), grad_inputs.astype(jnp.bfloat16), grad_skip.astype(jnp.bfloat16)))
    zero_grads = jax.tree.map(jnp.zeros_like, params)
    totals, outputs = lax.scan(one_pack, zero_grads, (frames, skip_frames, output_grad, labels_all, weighting_all))
    averaged = tuple((member / PACKS for member in totals))
    return (outputs[0], outputs[1], outputs[2], averaged[0], averaged[1], averaged[2], averaged[3], averaged[4], averaged[5], averaged[6], averaged[7], averaged[8], averaged[9], averaged[10], averaged[11], averaged[12])
```

```python
import functools
from types import SimpleNamespace

import jax
import jax.numpy as jnp
from jax import lax
from jax.experimental import pallas as pl
from jax.experimental.pallas import tpu as pltpu
from jax.sharding import PartitionSpec as P

HEADS = 8
HEAD_DIM = 64
EPSILON = 1e-05
LOG2E = 1.4426950408889634
AXES = ("gx", "gy")
RINGS = ("down", "up", "qkvw", "skipw")
RING_PARTS = ("_work", "_arrive", "_send", "_recv", "_free")
MESH = pl.DeviceIdType.MESH
VMEM_LIMIT = 67043328
f32, bf16 = jnp.float32, jnp.bfloat16
SKIP_B, GAIN1, SHIFT1, PROJ_B, GAIN2, SHIFT2, DOWN_B, UP_B = 0, 1, 2, 3, 4, 5, 6, 8


def nn(a, b):
    return lax.dot_general(a, b, (((1,), (0,)), ((), ())), preferred_element_type=f32)


def nt(a, b):
    return lax.dot_general(a, b, (((1,), (1,)), ((), ())), preferred_element_type=f32)


def tn(a, b):
    return lax.dot_general(a, b, (((0,), (0,)), ((), ())), preferred_element_type=f32)


def halves(pair):
    lane = lax.broadcasted_iota(jnp.int32, pair.shape, 1)
    zero = jnp.zeros_like(pair)
    return jnp.where(lane < HEAD_DIM, pair, zero), jnp.where(lane >= HEAD_DIM, pair, zero)


def row_stats(v):
    center = jnp.mean(v, axis=1, keepdims=True)
    offset = v - center
    inv = lax.rsqrt(jnp.mean(offset * offset, axis=1, keepdims=True) + EPSILON)
    return offset * inv, inv


def norm_backward(e, gain, xhat, inv):
    eg = e * gain
    return inv * (
        eg - jnp.mean(eg, axis=1, keepdims=True) - xhat * jnp.mean(eg * xhat, axis=1, keepdims=True)
    )


def colsum(v):
    return jnp.sum(v, axis=0, keepdims=True)


def device(d, ny):
    return (d // ny, lax.rem(d, ny))


def my_index(ny):
    return lax.axis_index("gx") * ny + lax.axis_index("gy")


def announce(me, n, ny):
    barrier = pltpu.get_barrier_semaphore()
    for k in range(1, n):
        pl.semaphore_signal(
            barrier, inc=1, device_id=device(jnp.bitwise_xor(me, k), ny), device_id_type=MESH
        )


def await_all(n):
    pl.semaphore_wait(pltpu.get_barrier_semaphore(), n - 1)


def partner_order(n):
    return sorted(range(1, n), key=lambda k: (-(k & 4), k))


class Exchange:
    def __init__(self, me, n, ny, source, target, sems):
        self.me, self.n, self.ny = me, n, ny
        self.source, self.target = source, target
        self.send, self.recv, self.local = (sems.at[i] for i in range(3))
        self.slots = source.shape[0] // n

    def block(self, d):
        return pl.ds(pl.multiple_of(d * self.slots, self.slots), self.slots)

    def copy(self, d):
        return pltpu.make_async_remote_copy(
            src_ref=self.source.at[self.block(d)],
            dst_ref=self.target.at[self.block(self.me)],
            send_sem=self.send,
            recv_sem=self.recv,
            device_id=device(d, self.ny),
            device_id_type=MESH,
        )

    def own(self):
        return pltpu.make_async_copy(
            self.source.at[self.block(self.me)], self.target.at[self.block(self.me)], self.local
        )

    def start(self):
        for k in partner_order(self.n):
            self.copy(jnp.bitwise_xor(self.me, k)).start()
        self.own().start()

    def wait(self):
        self.own().wait()
        every = pltpu.make_async_remote_copy(
            src_ref=self.source.at[pl.ds(0, self.slots * (self.n - 1))],
            dst_ref=self.target.at[pl.ds(0, self.slots * (self.n - 1))],
            send_sem=self.send,
            recv_sem=self.recv,
            device_id=device(self.me, self.ny),
            device_id_type=MESH,
        )
        every.wait_send()
        every.wait_recv()


class SmallSum:
    def __init__(self, me, n, ny, acc, slots, send, recv):
        self.me, self.n, self.ny = me, n, ny
        self.acc, self.slots, self.send, self.recv = acc, slots, send, recv
        self.levels = n.bit_length() - 1

    def copy(self, level):
        return pltpu.make_async_remote_copy(
            src_ref=self.acc.at[level],
            dst_ref=self.slots.at[level],
            send_sem=self.send.at[level],
            recv_sem=self.recv.at[level],
            device_id=device(jnp.bitwise_xor(self.me, 1 << level), self.ny),
            device_id_type=MESH,
        )

    def start(self, level):
        self.copy(level).start()

    def finish(self, level):
        self.copy(level).wait_recv()
        self.acc[level + 1] = self.acc[level] + self.slots[level]

    def drain(self):
        for level in range(self.levels):
            self.copy(level).wait_send()

    def run(self):
        for level in range(self.levels):
            self.start(level)
            self.finish(level)
        self.drain()


def ring_count(rows, n):
    return 2 if rows % (16 * n) == 0 else 1


def padded(rows, n):
    return rows + (-rows) % (8 * n)


class Ring:
    def __init__(self, me, n, ny, work, arrive, send, recv, free):
        self.me, self.n, self.ny = me, n, ny
        self.work, self.arrive = work, arrive
        self.send, self.recv, self.free = send, recv, free
        self.levels = n.bit_length() - 1
        self.steps = 2 * self.levels - 1
        high = list(range(3, self.levels))
        orders = ([0] + high + [1, 2], [0] + high[::-1] + [1, 2])
        rows = work.shape[0]
        self.parts = ring_count(rows, n)
        self.spans = []
        for h in range(self.parts):
            size = rows // self.parts
            offset = slot = h * size
            spans = []
            for level in range(self.levels):
                bit = orders[h][level]
                peer = jnp.bitwise_xor(me, 1 << bit)
                if level == self.levels - 1:
                    spans.append((offset, offset, size, slot, peer))
                    break
                size //= 2
                mine = jnp.bitwise_and(jnp.right_shift(me, bit), 1)
                keep = pl.multiple_of(offset + mine * size, 8)
                give = pl.multiple_of(offset + (1 - mine) * size, 8)
                spans.append((keep, give, size, slot, peer))
                offset, slot = keep, slot + size
            self.spans.append(spans)
        self.step = 0

    def level(self, step):
        return min(step, self.steps - 1 - step)

    def copy(self, h, step):
        keep, give, size, slot, peer = self.spans[h][self.level(step)]
        if step < self.levels:
            source, target = self.work.at[pl.ds(give, size)], self.arrive.at[pl.ds(slot, size)]
        else:
            source = target = self.work.at[pl.ds(keep, size)]
        return pltpu.make_async_remote_copy(
            src_ref=source,
            dst_ref=target,
            send_sem=self.send.at[h, step],
            recv_sem=self.recv.at[h, step],
            device_id=device(peer, self.ny),
            device_id_type=MESH,
        )

    def start(self, h, step):
        if step >= self.levels:
            pl.semaphore_wait(self.free.at[h, self.level(step)], 1)
        self.copy(h, step).start()

    def begin(self):
        for h in range(self.parts):
            self.start(h, 0)

    def advance(self):
        step = self.step
        self.step += 1
        for h in range(self.parts):
            copy = self.copy(h, step)
            copy.wait_recv()
            if step < self.levels:
                copy.wait_send()
                if step < self.levels - 1:
                    peer = self.spans[h][step][4]
                    pl.semaphore_signal(
                        self.free.at[h, step], inc=1, device_id=device(peer, self.ny), device_id_type=MESH
                    )
                self.add(h, step)
            if step + 1 < self.steps:
                self.start(h, step + 1)

    def add(self, h, step):
        keep, _, size, slot, _ = self.spans[h][step]
        tile = 8
        while tile < 128 and size % (2 * tile) == 0:
            tile *= 2

        def add(i, carry):
            at = pl.ds(pl.multiple_of(keep + i * tile, 8), tile)
            here = pl.ds(pl.multiple_of(slot + i * tile, 8), tile)
            self.work[at, :] = (self.work[at, :].astype(f32) + self.arrive[here, :].astype(f32)).astype(bf16)
            return carry

        lax.fori_loop(0, size // tile, add, 0)

    def drain(self):
        for h in range(self.parts):
            for step in range(self.levels, self.steps):
                self.copy(h, step).wait_send()


VM = pl.BlockSpec(memory_space=pltpu.VMEM)
HB = pl.BlockSpec(memory_space=pl.ANY)


def rows_at(i, tile):
    return pl.ds(pl.multiple_of(i * tile, tile), tile)


def loop(count, body, carry=0):
    return lax.fori_loop(0, count, body, carry)


def on(index, actions):
    for i, action in enumerate(actions):
        if action:
            pl.when(index == i)(lambda action=action: action())


def layer_kernel(n, ny, names, *refs):
    r = SimpleNamespace(**dict(zip(names, refs, strict=True)))
    me = my_index(ny)
    announce(me, n, ny)
    rows, width = r.stream.shape
    wide = r.up_w.shape[1]
    sem = r.sems

    def load(i, source, target):
        return pltpu.make_async_copy(source, target, sem.at[i])

    weights = SimpleNamespace(
        qkv_w=load(0, r.qkv_w_hbm, r.qkv_w), up_w=load(1, r.up_w_hbm, r.up_w), down_w=load(2, r.down_w_hbm, r.down_w),
        proj_w=load(3, r.proj_w_hbm, r.proj_w),
    )
    for copy in vars(weights).values():
        copy.start()

    tile = 256

    def project(i, carry):
        at = rows_at(i, tile)
        r.stream_out[at, :] = (
            nn(r.frames[at, :], r.skip_w[0:width, :])
            + nn(r.skip[at, :], r.skip_w[width:2 * width, :])
            + r.skip_b[...]
        ).astype(bf16)
        return carry

    loop(rows // tile, project)
    stream_move = Exchange(me, n, ny, r.stream_out, r.stream, r.move.at[0])
    grad_move = Exchange(me, n, ny, r.grad_hbm, r.grad, r.move.at[1])
    result_move = Exchange(me, n, ny, r.result, r.result_out, r.move.at[2])
    low_move = Exchange(me, n, ny, r.low_out, r.low, r.move.at[3])
    await_all(n)
    stream_move.start()

    count = SmallSum(me, n, ny, r.count_acc, r.count_slots, r.count_send, r.count_recv)
    r.count_acc[0] = r.count[...]
    count.run()
    factor = (n * rows) / r.count_acc[count.levels, 0:1, 0:1]
    meta_row = lax.broadcasted_iota(jnp.int32, (8, rows), 0)
    meta = jnp.where(meta_row == 2, r.meta[...] * factor, r.meta[...])
    r.columns[...] = jnp.transpose(jnp.concatenate([meta] * 16, axis=0))
    half = rows // 2

    def measure(i, carry):
        at = rows_at(i, tile)
        far = jnp.abs(
            i * tile + lax.broadcasted_iota(jnp.int32, (tile, rows), 0)
            - lax.broadcasted_iota(jnp.int32, (tile, rows), 1)
        ).astype(f32)
        same = r.columns[at, 0:1] == r.meta[0:1, :]
        r.distance[at, :] = jnp.where(same, far * LOG2E, 1e30)
        return carry

    loop(rows // tile, measure)
    r.small_acc[0] = jnp.zeros(r.small_acc.shape[1:], f32)

    def add_small(row, value):
        r.small_acc[0, row:row + 1, :] += value

    stream_move.wait()
    grad_move.start()

    weights.qkv_w.wait()

    def first(i, carry):
        at = rows_at(i, tile)
        xhat, _ = row_stats(r.stream[at, :].astype(f32))
        normed = (xhat * r.gain1[...] + r.shift1[...]).astype(bf16)
        r.normed1[at, :] = normed
        r.qkv[at, :] = nn(normed, r.qkv_w[...]).astype(bf16)
        return carry

    loop(rows // tile, first)
    scale = HEAD_DIM ** -0.5
    lane = lax.broadcasted_iota(jnp.int32, (half, 128), 1)

    def pair_cols(hp, which):
        return pl.ds(pl.multiple_of(which * width + hp * 128, 128), 128)

    def attend(hp, slope):
        key = r.qkv[:, pair_cols(hp, 1)]
        values = halves(r.qkv[:, pair_cols(hp, 2)])
        for q in range(2):
            at = slice(q * half, (q + 1) * half)
            queries = halves(r.qkv[at, pair_cols(hp, 0)])
            out = None
            for s in range(2):
                t = nt(queries[s], key) * (scale * LOG2E) - r.distance[at, :] * (slope * 0.5 ** s)
                top = jnp.max(t, axis=1, keepdims=True)
                p = jnp.exp2(t - top)
                summed = jnp.sum(p, axis=1, keepdims=True)
                part = nn(p.astype(bf16), values[s]) / summed
                out = part if out is None else out + part
                r.lse[at, :] = jnp.where(lane == 2 * hp + s, top + jnp.log2(summed), r.lse[at, :])
            r.blended[at, pair_cols(hp, 0)] = out.astype(bf16)
        return slope * 0.25

    loop(HEADS // 2, attend, jnp.float32(0.5))

    weights.proj_w.wait()
    weights.up_w.wait()
    weights.down_w.wait()
    grad_move.wait()

    def feed(i, carry):
        at = rows_at(i, tile)
        after = r.stream[at, :].astype(f32) + (nn(r.blended[at, :], r.proj_w[...]) + r.proj_b[...])
        xhat, _ = row_stats(after)
        r.after[at, :] = after
        low = (xhat * r.gain2[...] + r.shift2[...]).astype(bf16)
        r.normed2[at, :] = low
        pre = nn(low, r.up_w[...]) + r.up_b[...]
        cdf = 0.5 * (1.0 + lax.erf(pre * (2.0 ** -0.5)))
        act = (pre * cdf).astype(bf16)
        r.hidden[at, :] = act
        density = jnp.exp2(pre * pre * (-0.5 * LOG2E)) * 0.3989422804014327
        r.grad_pre[at, :] = (cdf + pre * density).astype(bf16)
        r.result[at, :] = (
            (after + (nn(act, r.down_w[...]) + r.down_b[...])) * r.columns[at, 1:2]
        ).astype(bf16)
        seed = (r.grad[at, :].astype(f32) * r.columns[at, 2:3]).astype(bf16)
        r.seed[at, :] = seed
        add_small(DOWN_B, colsum(seed.astype(f32)))
        return carry

    loop(rows // tile, feed)
    result_move.start()
    rings = SimpleNamespace()
    for name in RINGS:
        parts = (getattr(r, name + part) for part in RING_PARTS)
        setattr(rings, name, Ring(me, n, ny, *parts))

    def down_part(c, carry):
        r.down_work[rows_at(c, width), :] = tn(r.hidden[:, rows_at(c, width)], r.seed[...]).astype(bf16)
        return carry

    loop(wide // width, down_part)
    rings.down.begin()

    def feed_back(i, carry):
        at = rows_at(i, tile)
        grad_pre = (nt(r.seed[at, :], r.down_w[...]) * r.grad_pre[at, :].astype(f32)).astype(bf16)
        r.grad_pre[at, :] = grad_pre
        gn = nt(grad_pre, r.up_w[...])
        xhat, inv = row_stats(r.after[at, :])
        seed = r.grad[at, :].astype(f32) * r.columns[at, 2:3]
        after_grad = seed + norm_backward(gn, r.gain2[...], xhat, inv)
        r.after[at, :] = after_grad
        low = after_grad.astype(bf16)
        r.grad_blended[at, :] = nt(low, r.proj_w[...]).astype(bf16)
        add_small(GAIN2, colsum(gn * xhat))
        add_small(SHIFT2, colsum(gn))
        add_small(PROJ_B, colsum(low.astype(f32)))
        up_sum = colsum(grad_pre.astype(f32))
        for c in range(wide // width):
            add_small(UP_B + c, up_sum[:, c * width:(c + 1) * width])
        on(i, (None, rings.down.advance, None, rings.down.advance))
        return carry

    loop(rows // tile, feed_back)

    def up_part(c, carry):
        r.up_work[rows_at(c, width), :] = tn(r.normed2[...], r.grad_pre[:, rows_at(c, width)]).astype(bf16)
        return carry

    loop(wide // width, up_part)
    r.up_work[wide:wide + width, :] = tn(r.blended[...], r.after[...].astype(bf16)).astype(bf16)
    rings.up.begin()

    r.lse_rows[...] = jnp.transpose(r.lse[...])[0:8, :]
    group = lax.broadcasted_iota(jnp.int32, (8, width), 1) // HEAD_DIM
    pick = jnp.where(group == lax.broadcasted_iota(jnp.int32, (8, width), 0), 1.0, 0.0).astype(bf16)
    product = r.grad_blended[...].astype(f32) * r.blended[...].astype(f32)
    high = product.astype(bf16)
    r.delta[...] = nt(pick, high) + nt(pick, (product - high.astype(f32)).astype(bf16))

    def attend_back(hp, slope):
        key, value = r.qkv[:, pair_cols(hp, 1)], r.qkv[:, pair_cols(hp, 2)]
        keys = halves(key)
        grad_key = grad_value = None
        for q in range(2):
            at = slice(q * half, (q + 1) * half)
            queries = halves(r.qkv[at, pair_cols(hp, 0)])
            incomings = halves(r.grad_blended[at, pair_cols(hp, 0)])
            grad_query = None
            for s in range(2):
                head = pl.ds(2 * hp + s, 1)
                t = nt(key, queries[s]) * (scale * LOG2E) - r.distance[:, at] * (slope * 0.5 ** s)
                p = jnp.exp2(t - r.lse_rows[head, at])
                gp = nt(value, incomings[s])
                raw = (p * (gp - r.delta[head, at])).astype(bf16)
                value_part = nn(p.astype(bf16), incomings[s])
                key_part = nn(raw, queries[s])
                grad_value = value_part if grad_value is None else grad_value + value_part
                grad_key = key_part if grad_key is None else grad_key + key_part
                part = tn(keys[s], raw)
                grad_query = part if grad_query is None else grad_query + part
            r.qkv[at, pair_cols(hp, 0)] = (jnp.transpose(grad_query) * scale).astype(bf16)
            if q == 0:
                on(hp, (rings.up.advance,) * 4)
        r.qkv[:, pair_cols(hp, 1)] = (grad_key * scale).astype(bf16)
        r.qkv[:, pair_cols(hp, 2)] = grad_value.astype(bf16)
        on(hp, (rings.down.advance,) * 4)
        return slope * 0.25

    loop(HEADS // 2, attend_back, jnp.float32(0.5))

    def first_back(i, carry):
        at = rows_at(i, tile)
        gn = nt(r.qkv[at, :], r.qkv_w[...])
        xhat, inv = row_stats(r.stream[at, :].astype(f32))
        low = (r.after[at, :] + norm_backward(gn, r.gain1[...], xhat, inv)).astype(bf16)
        r.low_out[at, :] = low
        add_small(GAIN1, colsum(gn * xhat))
        add_small(SHIFT1, colsum(gn))
        add_small(SKIP_B, colsum(low.astype(f32)))
        return carry

    loop(rows // tile, first_back)
    low_move.start()

    def qkv_part(c, carry):
        r.qkvw_work[rows_at(c, width), :] = tn(r.normed1[...], r.qkv[:, rows_at(c, width)]).astype(bf16)
        return carry

    loop(3, qkv_part)
    rings.qkvw.begin()
    early = (rings.down, rings.up, rings.qkvw)
    small = SmallSum(me, n, ny, r.small_acc, r.small_slots, r.small_send, r.small_recv)
    for level in range(small.levels):
        small.start(level)
        for ring in early:
            if ring.step < ring.steps:
                ring.advance()
        small.finish(level)
    r.small_out[...] = r.small_acc[small.levels]
    low_move.wait()

    r.skipw_work[0:width, :] = tn(r.frames[...], r.low[...]).astype(bf16)
    r.skipw_work[width:2 * width, :] = tn(r.skip[...], r.low[...]).astype(bf16)
    rings.skipw.begin()

    def skip_back(i, carry):
        at = rows_at(i, tile)
        joined = nt(r.low[at, :], r.skip_w[...])
        r.hidden[at, 0:2 * width] = joined.astype(bf16)
        return carry

    loop(rows // tile, skip_back)
    outs = [
        pltpu.make_async_copy(r.hidden.at[:, pl.ds(i * width, width)], out, sem.at[4 + i])
        for i, out in enumerate((r.frames_out, r.skip_out))
    ]
    for copy in outs:
        copy.start()
    for ring, out in zip(early, (r.down_out, r.up_out, r.qkvw_out)):
        while ring.step < ring.steps:
            rings.skipw.advance() if rings.skipw.step < 2 else None
            ring.advance()
        outs.append(pltpu.make_async_copy(ring.work, out, sem.at[6 + len(outs)]))
        outs[-1].start()
    while rings.skipw.step < rings.skipw.steps:
        rings.skipw.advance()
    outs.append(pltpu.make_async_copy(r.skipw_work, r.skipw_out, sem.at[6 + len(outs)]))
    outs[-1].start()
    result_move.wait()
    small.drain()
    for ring in vars(rings).values():
        ring.drain()
    for copy in outs:
        copy.wait()


def pack_labels(lengths, assignment, frames_count, pack_id):
    in_pack = lengths * (assignment == pack_id).astype(jnp.int32)
    ends = jnp.cumsum(in_pack, dtype=jnp.int32)
    starts = ends - in_pack
    places = jnp.arange(frames_count, dtype=jnp.int32)
    inside = (places[None, :] >= starts[:, None]) & (places[None, :] < ends[:, None])
    numbers = jnp.arange(1, in_pack.shape[0] + 1, dtype=jnp.int32)
    return jnp.sum(jnp.where(inside, numbers[:, None], 0), axis=0)


def per_device(n, ny, frames, skip_frames, output_grad, lengths, assignment, infill, skip_weight,
               skip_bias, attn_gain, attn_shift, qkv_weight, proj_weight, proj_bias, ffn_gain,
               ffn_shift, up_weight, up_bias, down_weight, down_bias):
    slots, width = frames.shape[1], frames.shape[2]
    rows = n * slots
    wide = up_weight.shape[1]
    levels = n.bit_length() - 1
    me = lax.axis_index(AXES)
    labels = pack_labels(lengths, assignment, rows, me)
    valid = (labels > 0).astype(f32)
    weighting = infill[0].astype(f32) * valid
    count = jnp.broadcast_to(jnp.sum(weighting), (8, 128))
    label_row = labels.astype(f32)
    meta = jnp.stack([label_row, valid, weighting] + [valid] * 5)
    row = lambda v: v.reshape(1, -1)
    flat = lambda v: v.reshape(rows, width)

    ring_rows = dict(down=wide, up=wide + width, qkvw=3 * width, skipw=2 * width)
    ring_rows = {name: padded(size, n) for name, size in ring_rows.items()}
    ins = dict(
        frames=(VM, flat(frames)), skip=(VM, flat(skip_frames)), grad_hbm=(HB, flat(output_grad)),
        count=(VM, count), meta=(VM, meta), skip_w=(VM, skip_weight), skip_b=(VM, row(skip_bias)),
        gain1=(VM, row(attn_gain)), shift1=(VM, row(attn_shift)), qkv_w_hbm=(HB, qkv_weight),
        proj_w_hbm=(HB, proj_weight), proj_b=(VM, row(proj_bias)), gain2=(VM, row(ffn_gain)),
        shift2=(VM, row(ffn_shift)), up_w_hbm=(HB, up_weight), up_b=(VM, row(up_bias)),
        down_w_hbm=(HB, down_weight), down_b=(VM, row(down_bias)),
    )
    outs = dict(
        result_out=(HB, (rows, width), bf16), frames_out=(HB, (rows, width), bf16),
        skip_out=(HB, (rows, width), bf16), small_out=(VM, (16, width), f32),
    )
    for name, size in ring_rows.items():
        outs[name + "_out"] = (HB, (size, width), bf16)
    one = ((rows, width), bf16)
    buffers = dict(
        stream_out=one, stream=one, grad=one, normed1=one, blended=one, normed2=one,
        seed=one, result=one, grad_blended=one, low_out=one, low=one,
        qkv=((rows, 3 * width), bf16), hidden=((rows, wide), bf16), grad_pre=((rows, wide), bf16),
        after=((rows, width), f32), distance=((rows, rows), f32), columns=((rows, 128), f32),
        lse=((rows, 128), f32), lse_rows=((8, rows), f32), delta=((8, rows), f32),
        qkv_w=(qkv_weight.shape, bf16), proj_w=(proj_weight.shape, bf16),
        up_w=(up_weight.shape, bf16), down_w=(down_weight.shape, bf16),
    )
    for name, size in ring_rows.items():
        buffers[name + "_work"] = ((size, width), bf16)
        buffers[name + "_arrive"] = ((size, width), bf16)
    for name, shape in (("count", (8, 128)), ("small", (16, width))):
        buffers[name + "_acc"] = ((levels + 1, *shape), f32)
        buffers[name + "_slots"] = ((levels, *shape), f32)
    scratch = {name: pltpu.VMEM(*spec) for name, spec in buffers.items()}
    for name in ("count", "small"):
        scratch[name + "_send"] = scratch[name + "_recv"] = pltpu.SemaphoreType.DMA((levels,))
    for name, size in ring_rows.items():
        shape = (ring_count(size, n), 2 * levels - 1)
        scratch[name + "_send"] = scratch[name + "_recv"] = pltpu.SemaphoreType.DMA(shape)
        scratch[name + "_free"] = pltpu.SemaphoreType.REGULAR((ring_count(size, n), levels - 1))
    scratch["sems"] = pltpu.SemaphoreType.DMA((12,))
    scratch["move"] = pltpu.SemaphoreType.DMA((4, 3))

    got = pl.pallas_call(
        functools.partial(layer_kernel, n, ny, [*ins, *outs, *scratch]),
        out_shape=tuple(jax.ShapeDtypeStruct(shape, kind) for _, shape, kind in outs.values()),
        in_specs=[spec for spec, _ in ins.values()],
        out_specs=tuple(spec for spec, _, _ in outs.values()),
        scratch_shapes=list(scratch.values()),
        compiler_params=pltpu.CompilerParams(
            vmem_limit_bytes=VMEM_LIMIT, collective_id=0, has_side_effects=True
        ),
        name="layer",
    )(*(value for _, value in ins.values()))
    got = SimpleNamespace(**dict(zip(outs, got)))

    def mean(v):
        return v.astype(f32) / n

    def side(v):
        return jnp.concatenate([v[c * width:(c + 1) * width] for c in range(v.shape[0] // width)], axis=1)

    small = got.small_out / n
    split = lambda v: v.reshape(frames.shape)
    return (
        split(got.result_out), split(got.frames_out), split(got.skip_out),
        mean(got.skipw_out[:2 * width]), small[SKIP_B], small[GAIN1], small[SHIFT1],
        mean(side(got.qkvw_out[:3 * width])), mean(got.up_out[wide:wide + width]), small[PROJ_B],
        small[GAIN2], small[SHIFT2], mean(side(got.up_out[:wide])),
        small[UP_B:UP_B + wide // width].reshape(-1), mean(got.down_out[:wide]), small[DOWN_B],
    )


def solution(mesh):
    n, ny = mesh.size, mesh.shape["gy"]
    spread = P(None, AXES, None)
    return jax.shard_map(
        functools.partial(per_device, n, ny),
        mesh=mesh,
        in_specs=(spread,) * 3 + (P(), P(), P(AXES, None)) + (P(),) * 13,
        out_specs=(spread,) * 3 + (P(),) * 13,
        check_vma=False,
    )
```
